256 devices in a mesh: pipe: 4 (over x), seq: 64 (over y, z, core).
Axes of the slice: x: 4, y: 4, z: 8, core: 2. Of those that a mesh axis runs over, the one named last changes fastest.
Arguments:
- acts: bfloat16 [4, 16384, 1024], P('pipe', 'seq'), may hold values from -6 to 6
- cotan: bfloat16 [4, 16384, 1024], P('pipe', 'seq'), may hold values from -6 to 6
- proj_in: bfloat16 [4, 1024, 2048], P('pipe'), may hold values from -0.1875 to 0.1875
- proj_out: bfloat16 [4, 1024, 1024], P('pipe'), may hold values from -0.1875 to 0.1875
- block_mix: bfloat16 [4, 16384, 256], P('pipe', 'seq'), may hold values from -0.375 to 0.375
- twiddle: float32 [4, 6, 2, 2, 1024], P('pipe'), may hold values from -2.5 to 2.5
Outputs:
- mixed: bfloat16 [4, 16384, 1024], P('pipe', 'seq')
- grad_prev: bfloat16 [4, 16384, 1024], P('pipe', 'seq')
- grad_in_proj: float32 [4, 1024, 2048], P('pipe', 'seq')
- grad_out_proj: float32 [4, 1024, 1024], P('pipe', 'seq')
- grad_block_mix: float32 [4, 16384, 256], P('pipe', 'seq')
- grad_twiddle: float32 [4, 6, 2, 2, 1024], P('pipe')
The draws below stay inside these ranges and needn't reach their ends.
All inputs are finite; a program needn't handle non-finite values.
Results may differ from the reference program's by a relative error of at most 0.014.
Values may be sent and summed in bfloat16 or wider, within the bound.
A program may use at most 128 MiB of HBM per device.

```python
import jax
import jax.numpy as jnp

D = 1024
TOK_DEV = 256
SECTIONS = 4
LEN = 16384
BITS = 6
N_SEQ = 64


def levels(stream_key, extent, shards, smallest, top_value):
    loudness, own = 1.0, jax.random.fold_in(stream_key, 6)
    for axis_at, shards_of in shards:
        draws = jnp.exp(jax.random.uniform(jax.random.fold_in(own, axis_at), (shards_of,), jnp.float32, smallest / len(shards), top_value / len(shards)))
        loudness = loudness * jnp.repeat(draws, extent[axis_at] // shards_of).reshape([-1 if axis == axis_at else 1 for axis in range(len(extent))])
    return loudness


def normal_values(stream_key, shape, scale, reach, split=(), kind=jnp.bfloat16):
    drawn = jax.random.normal(stream_key, shape, jnp.float32) * scale
    if len(split) > 0:
        drawn = levels(stream_key, shape, split, -0.22, 0.18) * drawn
    return jnp.clip(drawn, min=-reach, max=reach).astype(kind)


def setup_inputs(seed: int = 0) -> dict:
    key_of = jax.random.split(jax.random.key(seed), 7)
    acts = normal_values(key_of[0], (SECTIONS, LEN, D), 1.0, 6.0, ((0, 4), (1, 64)))
    cotan = normal_values(key_of[1], (SECTIONS, LEN, D), 1.0, 6.0, ((0, 4), (1, 64)))
    proj_in = normal_values(key_of[2], (SECTIONS, D, 2 * D), D ** -0.5, 0.1875, ((0, 4),))
    proj_out = normal_values(key_of[3], (SECTIONS, D, D), D ** -0.5, 0.1875, ((0, 4),))
    block_mix = normal_values(key_of[4], (SECTIONS, LEN, TOK_DEV), TOK_DEV ** -0.5, 0.375, ((0, 4), (1, 64)))
    twiddle = normal_values(key_of[5], (SECTIONS, BITS, 2, 2, D), 0.7, 2.5, ((0, 4),), jnp.float32)
    return dict(acts=acts, cotan=cotan, proj_in=proj_in, proj_out=proj_out, block_mix=block_mix, twiddle=twiddle)


def local_segment(blocked, segment_coef, segment_bit):
    block_count, inner_rows, feature_count = blocked.shape
    stride_len = 2 ** segment_bit
    shaped = blocked.reshape(block_count // (2 * stride_len), 2, stride_len, inner_rows, feature_count)
    lower_part = shaped[:, 0].astype(jnp.float32)
    upper_part = shaped[:, 1].astype(jnp.float32)
    new_lower = segment_coef[0, 0] * lower_part + segment_coef[0, 1] * upper_part
    new_upper = segment_coef[1, 0] * upper_part + segment_coef[1, 1] * lower_part
    joined = jnp.stack([new_lower, new_upper], axis=1)
    return joined.reshape(block_count, inner_rows, feature_count).astype(jnp.bfloat16)


def local_back(grad_blocked, stored, segment_coef, segment_bit):
    block_count, inner_rows, feature_count = grad_blocked.shape
    stride_len = 2 ** segment_bit
    dshape = grad_blocked.reshape(block_count // (2 * stride_len), 2, stride_len, inner_rows, feature_count)
    zshape = stored.reshape(block_count // (2 * stride_len), 2, stride_len, inner_rows, feature_count)
    grad_lower = dshape[:, 0].astype(jnp.float32)
    grad_upper = dshape[:, 1].astype(jnp.float32)
    val_lower = zshape[:, 0].astype(jnp.float32)
    val_upper = zshape[:, 1].astype(jnp.float32)
    prev_lower = segment_coef[0, 0] * grad_lower + segment_coef[1, 1] * grad_upper
    prev_upper = segment_coef[1, 0] * grad_upper + segment_coef[0, 1] * grad_lower
    joined = jnp.stack([prev_lower, prev_upper], axis=1)
    prev = joined.reshape(block_count, inner_rows, feature_count).astype(jnp.bfloat16)
    axes_sum = (0, 1, 2)
    partial_value = jnp.stack([
        jnp.stack([jnp.sum(grad_lower * val_lower, axis=axes_sum), jnp.sum(grad_lower * val_upper, axis=axes_sum)]),
        jnp.stack([jnp.sum(grad_upper * val_upper, axis=axes_sum), jnp.sum(grad_upper * val_lower, axis=axes_sum)]),
    ])
    return prev, partial_value


def reference(acts, cotan, proj_in, proj_out, block_mix, twiddle):
    outs_mixed = []
    outs_dacts = []
    outs_win = []
    outs_wout = []
    outs_block = []
    outs_twid = []
    for section in range(SECTIONS):
        inputs = acts[section]
        grad_out = cotan[section]
        w_in = proj_in[section]
        w_out = proj_out[section]
        feature_count = inputs.shape[1]
        projected = jnp.dot(inputs, w_in, preferred_element_type=jnp.float32)
        value = projected[:, :feature_count].astype(jnp.bfloat16)
        gate = projected[:, feature_count:].astype(jnp.bfloat16)
        value_blocks = value.reshape(N_SEQ, TOK_DEV, feature_count)
        mats = block_mix[section].reshape(N_SEQ, TOK_DEV, TOK_DEV)
        blocked = jnp.einsum('pij,pjc->pic', mats.astype(jnp.float32), value_blocks.astype(jnp.float32)).astype(jnp.bfloat16)
        stored = []
        for segment_bit in range(BITS):
            stored.append(blocked)
            blocked = local_segment(blocked, twiddle[section, segment_bit], segment_bit)
        monarch = blocked.reshape(LEN, feature_count)
        hidden = (monarch.astype(jnp.float32) * gate.astype(jnp.float32)).astype(jnp.bfloat16)
        outs_mixed.append(jnp.dot(hidden, w_out, preferred_element_type=jnp.float32).astype(jnp.bfloat16))
        d_hidden = jnp.dot(grad_out, w_out.T, preferred_element_type=jnp.float32).astype(jnp.bfloat16)
        outs_wout.append(jnp.dot(hidden.T, grad_out, preferred_element_type=jnp.float32))
        d_monarch = (d_hidden.astype(jnp.float32) * gate.astype(jnp.float32)).astype(jnp.bfloat16)
        d_gate = (d_hidden.astype(jnp.float32) * monarch.astype(jnp.float32)).astype(jnp.bfloat16)
        grad_blocked = d_monarch.reshape(N_SEQ, TOK_DEV, feature_count)
        partials = [None] * BITS
        for segment_bit in range(BITS - 1, -1, -1):
            grad_blocked, partials[segment_bit] = local_back(grad_blocked, stored[segment_bit], twiddle[section, segment_bit], segment_bit)
        outs_twid.append(jnp.stack(partials))
        d_value = jnp.einsum('pij,pic->pjc', mats.astype(jnp.float32), grad_blocked.astype(jnp.float32)).astype(jnp.bfloat16)
        grad_mats = jnp.einsum('pic,pjc->pij', grad_blocked.astype(jnp.float32), value_blocks.astype(jnp.float32))
        outs_block.append(grad_mats.reshape(LEN, TOK_DEV))
        d_projected = jnp.concatenate([d_value.reshape(LEN, feature_count), d_gate], axis=1)
        outs_win.append(jnp.dot(inputs.T, d_projected, preferred_element_type=jnp.float32))
        outs_dacts.append(jnp.dot(d_projected, w_in.T, preferred_element_type=jnp.float32).astype(jnp.bfloat16))
    handed = outs_dacts[1:] + [jnp.zeros_like(outs_dacts[0])]
    return (jnp.stack(outs_mixed), jnp.stack(handed), jnp.stack(outs_win), jnp.stack(outs_wout), jnp.stack(outs_block), jnp.stack(outs_twid))
```

```python
import functools

import jax
import jax.numpy as jnp
from jax import lax
from jax.experimental import pallas as pl
from jax.experimental.pallas import tpu as pltpu
from jax.sharding import PartitionSpec as P

F32 = jnp.float32
BF16 = jnp.bfloat16
MESH = pl.DeviceIdType.MESH
HALVES = 2
LANES = 128


def ring_sizes(count):
    bits = count.bit_length() - 2
    y_bits = bits // 2
    return 1 << y_bits, 1 << (bits - y_bits)


def butterfly(parts, coefs):
    stages = [parts]
    for bit, coef in enumerate(coefs):
        now = stages[-1]
        after = [None] * len(now)
        for low in range(len(now)):
            high = low | 1 << bit
            if high != low:
                after[low] = coef[0] * now[low] + coef[1] * now[high]
                after[high] = coef[2] * now[high] + coef[3] * now[low]
        stages.append(after)
    return stages


def butterfly_back(grads, coefs):
    stages = [grads]
    for bit in range(len(coefs) - 1, -1, -1):
        coef = coefs[bit]
        now = stages[0]
        before = [None] * len(now)
        for low in range(len(now)):
            high = low | 1 << bit
            if high != low:
                before[low] = coef[0] * now[low] + coef[3] * now[high]
                before[high] = coef[2] * now[high] + coef[1] * now[low]
        stages.insert(0, before)
    return stages


def coef_grads(stages, grad_stages, bits):
    totals = []
    for bit in range(bits):
        vals, grads = stages[bit], grad_stages[bit + 1]
        sums = [None] * 4
        for low in range(len(vals)):
            high = low | 1 << bit
            if high != low:
                terms = (
                    grads[low] * vals[low],
                    grads[low] * vals[high],
                    grads[high] * vals[high],
                    grads[high] * vals[low],
                )
                sums = [t if s is None else s + t for s, t in zip(sums, terms)]
        totals += [jnp.sum(s, axis=0, keepdims=True) for s in sums]
    return totals


class Links:
    def __init__(self, ny, nz, send, recv):
        self.ny, self.nz = ny, nz
        self.send, self.recv = send, recv
        self.used = 0
        self.copies = []
        me = lax.axis_index("seq")
        self.c = lax.rem(me, 2)
        self.z = lax.rem(me // 2, nz)
        self.y = me // (2 * nz)

    def seq(self, y, z, c):
        return (y * self.nz + z) * 2 + c

    def z_peer(self, apart):
        return lax.rem(self.z + apart + self.nz, self.nz)

    def y_peer(self, apart):
        return lax.rem(self.y + apart + self.ny, self.ny)

    def put(self, source, target, y, z, c):
        copy = pltpu.make_async_remote_copy(
            src_ref=source,
            dst_ref=target,
            send_sem=self.send.at[self.used],
            recv_sem=self.recv.at[self.used],
            device_id={"seq": self.seq(y, z, c)},
            device_id_type=MESH,
        )
        copy.start()
        self.used += 1
        self.copies.append(copy)
        return copy

    def greet(self):
        barrier = pltpu.get_barrier_semaphore()
        count = 0
        for apart in range(1, self.nz):
            pl.semaphore_signal(
                barrier, inc=1, device_id={"seq": self.seq(self.y, self.z_peer(apart), self.c)}, device_id_type=MESH
            )
            count += 1
        for apart in range(1, self.ny):
            pl.semaphore_signal(
                barrier, inc=1, device_id={"seq": self.seq(self.y_peer(apart), self.z, self.c)}, device_id_type=MESH
            )
            count += 1
        pl.semaphore_signal(
            barrier, inc=1, device_id={"seq": self.seq(self.y, self.z, 1 - self.c)}, device_id_type=MESH
        )
        return barrier, count + 1


def arrived(copies):
    for copy in copies:
        copy.wait_recv()


def mixer_copies(ny, nz):
    return 4 * HALVES * (nz - 1) + 4 * HALVES * (ny - 1) + 2 * HALVES


def mixer_kernel(
    ny, nz, seg0, dseg6, tw, monarch, dseg0, gtw,
    fzin, fzout, fy0, fyin, fyout, fc0, fcin, bcin, by0, byin, byout, bz0, bzin, bzout, send, recv,
):
    links = Links(ny, nz, send, recv)
    y, z, c = links.y, links.z, links.c
    per_y = nz // ny
    z_bits, y_bits = nz.bit_length() - 1, ny.bit_length() - 1
    tiles = seg0.shape[-1] // LANES
    barrier, greeted = links.greet()
    pl.semaphore_wait(barrier, greeted)

    def lanes_of(tile):
        return pl.ds(pl.multiple_of(tile * LANES, LANES), LANES)

    def coefs_of(first_bit, bits, lanes):
        return [[tw[pl.ds((first_bit + b) * 4 + k, 1), lanes] for k in range(4)] for b in range(bits)]

    def z_out(source, target, h):
        target[h, z] = source[h, z]
        return [
            links.put(source.at[h, links.z_peer(p)], target.at[h, z], y, links.z_peer(p), c) for p in range(1, nz)
        ]

    def z_back(source, target, h):
        target[h, z] = source[h, z]
        return [
            links.put(source.at[h, links.z_peer(p)], target.at[h, z], y, links.z_peer(p), c) for p in range(1, nz)
        ]

    def rows_y(which):
        return pl.ds(which * per_y, per_y)

    def y_out(source, target, h):
        target[h, y] = source[h, rows_y(y)]
        return [
            links.put(source.at[h, rows_y(links.y_peer(p))], target.at[h, y], links.y_peer(p), z, c)
            for p in range(1, ny)
        ]

    def y_back(source, target, h):
        target[h, rows_y(y)] = source[h, y]
        return [
            links.put(source.at[h, links.y_peer(p)], target.at[h, rows_y(y)], links.y_peer(p), z, c)
            for p in range(1, ny)
        ]

    def f_z(h):
        @pl.loop(0, tiles)
        def _(tile):
            lanes = lanes_of(tile)
            coefs = coefs_of(1, z_bits, lanes)
            out = butterfly([fzin[h, k, :, lanes].astype(F32) for k in range(nz)], coefs)[-1]
            for k in range(nz):
                fzout[h, k, :, lanes] = out[k].astype(BF16)

    def b_y(h):
        @pl.loop(0, tiles)
        def _(tile):
            lanes = lanes_of(tile)
            coefs = coefs_of(1 + z_bits, y_bits, lanes)
            for r in range(per_y):
                out = butterfly_back([byin[h, k, r, :, lanes].astype(F32) for k in range(ny)], coefs)[0]
                for k in range(ny):
                    byout[h, k, r, :, lanes] = out[k].astype(BF16)

    def add_grads(tile, first_bit, totals):
        for k, total in enumerate(totals):
            row = pl.ds(first_bit * 4 + k, 1)
            gtw[tile, row, :] = gtw[tile, row, :] + total

    def f_y(h):
        @pl.loop(0, tiles)
        def _(tile):
            lanes = lanes_of(tile)
            coefs = coefs_of(1 + z_bits, y_bits, lanes)
            for r in range(per_y):
                stages = butterfly([fyin[h, k, r, :, lanes].astype(F32) for k in range(ny)], coefs)
                grads = butterfly_back([byin[h, k, r, :, lanes].astype(F32) for k in range(ny)], coefs)
                for k in range(ny):
                    fyout[h, k, r, :, lanes] = stages[-1][k].astype(BF16)
                add_grads(tile, 1 + z_bits, coef_grads(stages, grads, y_bits))

    def b_z(h):
        @pl.loop(0, tiles)
        def _(tile):
            lanes = lanes_of(tile)
            coefs = coefs_of(1, z_bits, lanes)
            stages = butterfly([fzin[h, k, :, lanes].astype(F32) for k in range(nz)], coefs)
            grads = butterfly_back([bzin[h, k, :, lanes].astype(F32) for k in range(nz)], coefs)
            for k in range(nz):
                bzout[h, k, :, lanes] = grads[0][k].astype(BF16)
            add_grads(tile, 1, coef_grads(stages, grads, z_bits))

    def b_core(h):
        @pl.loop(0, tiles)
        def _(tile):
            lanes = lanes_of(tile)
            own = jnp.where(c == 0, tw[pl.ds(0, 1), lanes], tw[pl.ds(2, 1), lanes])
            peer = jnp.where(c == 0, tw[pl.ds(3, 1), lanes], tw[pl.ds(1, 1), lanes])
            for k in range(nz):
                by0[h, k, :, lanes] = (
                    own * dseg6[h, k, :, lanes].astype(F32) + peer * bcin[h, k, :, lanes].astype(F32)
                ).astype(BF16)

    def f_core(h):
        @pl.loop(0, tiles)
        def _(tile):
            lanes = lanes_of(tile)
            own = jnp.where(c == 0, tw[pl.ds(0, 1), lanes], tw[pl.ds(2, 1), lanes])
            peer = jnp.where(c == 0, tw[pl.ds(1, 1), lanes], tw[pl.ds(3, 1), lanes])
            sums = [None, None]
            for k in range(nz):
                mine = fc0[h, k, :, lanes].astype(F32)
                other = fcin[h, k, :, lanes].astype(F32)
                grad = dseg6[h, k, :, lanes].astype(F32)
                monarch[h, k, :, lanes] = (own * mine + peer * other).astype(BF16)
                terms = (grad * mine, grad * other)
                sums = [t if s is None else s + t for s, t in zip(sums, terms)]
            for k in range(4):
                total = jnp.sum(sums[k % 2], axis=0, keepdims=True)
                row = pl.ds(k, 1)
                gtw[tile, row, :] = gtw[tile, row, :] + jnp.where(c == k // 2, total, 0.0)

    both = range(HALVES)
    fz = [z_out(seg0, fzin, h) for h in both]
    bc = [links.put(dseg6.at[h], bcin.at[h], y, z, 1 - c) for h in both]
    gtw[...] = jnp.zeros_like(gtw)
    by = []
    for h in both:
        bc[h].wait_recv()
        b_core(h)
        by.append(y_out(by0, byin, h))
    fzb, byb = [], []
    for h in both:
        arrived(fz[h])
        f_z(h)
        fzb.append(z_back(fzout, fy0, h))
        arrived(by[h])
        b_y(h)
        byb.append(y_back(byout, bz0, h))
    bz = []
    for h in both:
        arrived(byb[h])
        bz.append(z_out(bz0, bzin, h))
    fy = []
    for h in both:
        arrived(fzb[h])
        fy.append(y_out(fy0, fyin, h))
    fyb = []
    for h in both:
        arrived(fy[h])
        f_y(h)
        fyb.append(y_back(fyout, fc0, h))
    fc, bzb = [], []
    for h in both:
        arrived(fyb[h])
        fc.append(links.put(fc0.at[h], fcin.at[h], y, z, 1 - c))
        if h == 0:
            arrived(bz[h])
            b_z(h)
            bzb.append(z_back(bzout, dseg0, h))
    for h in both:
        fc[h].wait_recv()
        f_core(h)
    for h in both:
        if h > 0:
            arrived(bz[h])
            b_z(h)
            bzb.append(z_back(bzout, dseg0, h))
    for h in both:
        arrived(bzb[h])
    for copy in links.copies:
        copy.wait_send()


def mixer(ny, nz, seg0, dseg6, tw):
    rows, width = seg0.shape
    inner = rows // (HALVES * nz)
    per_y = nz // ny
    tiles = width // LANES
    shape_z = (HALVES, nz, inner, width)
    shape_y = (HALVES, ny, per_y, inner, width)
    count = mixer_copies(ny, nz)
    vmem = pl.BlockSpec(memory_space=pltpu.VMEM)
    kinds = [
        shape_z, shape_z, shape_z, shape_y, shape_y, shape_z, shape_z,
        shape_z, shape_z, shape_y, shape_y, shape_z, shape_z, shape_z,
    ]
    monarch, dseg0, gtw = pl.pallas_call(
        functools.partial(mixer_kernel, ny, nz),
        out_shape=(
            jax.ShapeDtypeStruct(shape_z, BF16),
            jax.ShapeDtypeStruct(shape_z, BF16),
            jax.ShapeDtypeStruct((tiles, tw.shape[0], LANES), F32),
        ),
        in_specs=[vmem] * 3,
        out_specs=(vmem,) * 3,
        scratch_shapes=[pltpu.VMEM(shape, BF16) for shape in kinds]
        + [pltpu.SemaphoreType.DMA((count,)), pltpu.SemaphoreType.DMA((count,))],
        compiler_params=pltpu.CompilerParams(collective_id=0, has_side_effects=True),
        name="mixer",
    )(seg0.reshape(shape_z), dseg6.reshape(shape_z), tw)
    return monarch.reshape(rows, width), dseg0.reshape(rows, width), gtw


class Chain:
    def __init__(self, size, me, way, steps, own, come, go, ship):
        self.size, self.me, self.way, self.steps = size, me, way, steps
        self.own, self.come, self.go, self.ship = own, come, go, ship
        self.copy = None

    def step(self, at):
        if at >= self.steps:
            return
        dest = lax.rem(self.me + self.way * (self.steps - at) + self.size, self.size)
        source = self.own.at[dest]
        if at > 0:
            self.copy.wait_recv()
            self.go[at - 1] = (self.own[dest].astype(F32) + self.come[at - 1].astype(F32)).astype(BF16)
            source = self.go.at[at - 1]
        self.copy = self.ship(source, self.come.at[at], self.way)

    def last(self):
        if self.steps == 0:
            return None
        self.copy.wait_recv()
        return self.come[self.steps - 1].astype(F32)


def chains_of(size, me, own, come, go, ship):
    longer, shorter = size // 2, size // 2 - 1
    pairs = []
    for part, (ahead, behind) in enumerate(((longer, shorter), (shorter, longer))):
        pairs.append(
            [
                Chain(size, me, 1, ahead, own[part], come[part][0], go[part][0], ship),
                Chain(size, me, -1, behind, own[part], come[part][1], go[part][1], ship),
            ]
        )
    return pairs


def settled(pair, own, me):
    total = own[me].astype(F32)
    for chain in pair:
        value = chain.last()
        if value is not None:
            total = total + value
    return total


def ring_steps(pairs, at):
    for pair in pairs:
        for chain in pair:
            chain.step(at)


def sums_copies(ny, nz):
    return 2 * ((ny - 1) + (nz - 1)) * 2 + 2 * (nz - 1) + (ny - 1) + 2


def sums_kernel(
    ny, nz, c1, cg, cw, gtw, grad_in, win, wout, tw_out, handed,
    z1come, z1go, y1own, y1come, y1go, y2come, y2go, z2own, z2come, z2go,
    tz_in, ty_in, tc_in, tsum, tall, fin, fin_in, send, recv, hand_send, hand_recv,
):
    links = Links(ny, nz, send, recv)
    y, z, c = links.y, links.z, links.c
    pipe = lax.axis_index("pipe")
    pipes = lax.axis_size("pipe")
    barrier, greeted = links.greet()
    for apart in (1, pipes - 1):
        pl.semaphore_signal(
            barrier, inc=1, device_id={"pipe": lax.rem(pipe + apart, pipes)}, device_id_type=MESH
        )
    pl.semaphore_wait(barrier, greeted + 2)

    def hand_copy(target):
        return pltpu.make_async_remote_copy(
            src_ref=grad_in,
            dst_ref=handed,
            send_sem=hand_send,
            recv_sem=hand_recv,
            device_id={"pipe": target},
            device_id_type=MESH,
        )

    @pl.when(pipe > 0)
    def _():
        hand_copy(pipe - 1).start()

    @pl.when(pipe == pipes - 1)
    def _():
        handed[...] = jnp.zeros_like(handed)

    def ship_z(source, target, way):
        return links.put(source, target, y, links.z_peer(way), c)

    def ship_y(source, target, way):
        return links.put(source, target, links.y_peer(way), z, c)

    def halves_of(ref):
        return [[ref.at[part, way] for way in range(2)] for part in range(2)]

    c1_own = [c1.at[0], c1.at[1]]
    first = chains_of(nz, z, c1_own, halves_of(z1come), halves_of(z1go), ship_z)
    c2_own = [cg, cw]
    second = chains_of(ny, y, c2_own, halves_of(y2come), halves_of(y2go), ship_y)
    ring_steps(first, 0)
    ring_steps(second, 0)
    tz = [links.put(gtw.at[links.z_peer(p)], tz_in.at[p - 1], y, links.z_peer(p), c) for p in range(1, nz)]
    z_steps, y_steps = nz // 2, ny // 2
    ring_steps(first, 1)
    arrived(tz)
    total = gtw[z]
    for p in range(nz - 1):
        total = total + tz_in[p]
    tsum[0] = total
    ty = [links.put(tsum.at[0], ty_in.at[p - 1], links.y_peer(p), z, c) for p in range(1, ny)]
    ring_steps(second, 1)
    for at in range(2, z_steps):
        ring_steps(first, at)
    for at in range(2, y_steps):
        ring_steps(second, at)
    arrived(ty)
    total = tsum[0]
    for p in range(ny - 1):
        total = total + ty_in[p]
    tsum[1] = total
    tc = links.put(tsum.at[1], tc_in, y, z, 1 - c)
    for part in range(2):
        y1own[part] = settled(first[part], c1_own[part], z).astype(BF16)
    y1 = chains_of(ny, y, [y1own.at[0], y1own.at[1]], halves_of(y1come), halves_of(y1go), ship_y)
    ring_steps(y1, 0)
    for part in range(2):
        z2own[part] = settled(second[part], c2_own[part], y).astype(BF16)
    z2 = chains_of(nz, z, [z2own.at[0], z2own.at[1]], halves_of(z2come), halves_of(z2go), ship_z)
    ring_steps(z2, 0)
    tc.wait_recv()
    tall[z] = tsum[1] + tc_in[...]
    ta = [links.put(tall.at[z], tall.at[z], y, links.z_peer(p), c) for p in range(1, nz)]
    for at in range(1, y_steps):
        ring_steps(y1, at)
    for at in range(1, z_steps):
        ring_steps(z2, at)
    v_part = y1own.shape[-1]
    o_part = z2own.shape[-1]
    for part in range(2):
        fin[:, part * v_part : (part + 1) * v_part] = settled(y1[part], y1own.at[part], y)
    for part in range(2):
        start = 2 * v_part + part * o_part
        fin[:, start : start + o_part] = settled(z2[part], z2own.at[part], z)
    mine = win.shape[0]
    fc = links.put(fin.at[pl.ds(mine * (1 - c), mine)], fin_in, y, z, 1 - c)
    arrived(ta)
    for k in range(nz):
        tw_out[:, k * LANES : (k + 1) * LANES] = tall[k]
    width = win.shape[1] // 2
    half = width // 2

    def lay(rows_of, core):
        win[:, pl.ds(pl.multiple_of(core * half, half), half)] = rows_of(0, half)
        win[:, pl.ds(pl.multiple_of(width + core * half, half), half)] = rows_of(half, half)
        wout[:, pl.ds(pl.multiple_of(core * half, half), half)] = rows_of(2 * half, half)

    lay(lambda start, size: fin[pl.ds(mine * c, mine), pl.ds(start, size)], c)
    fc.wait_recv()
    lay(lambda start, size: fin_in[:, pl.ds(start, size)], 1 - c)
    for copy in links.copies:
        copy.wait_send()

    @pl.when(pipe < pipes - 1)
    def _():
        hand_copy(pipe).wait_recv()

    @pl.when(pipe > 0)
    def _():
        hand_copy(pipe - 1).wait_send()


def sums(ny, nz, c1, cg, cw, gtw, grad_in):
    block, v_part = c1.shape[-2:]
    o_part = cg.shape[-1]
    width = 4 * v_part
    own_rows = block // 2
    tiles, tw_rows, _ = gtw.shape
    count = sums_copies(ny, nz)
    vmem = pl.BlockSpec(memory_space=pltpu.VMEM)
    z_steps, y_steps = nz // 2, ny // 2
    scratch = [
        pltpu.VMEM((2, 2, z_steps, ny, block, v_part), BF16),
        pltpu.VMEM((2, 2, z_steps, ny, block, v_part), BF16),
        pltpu.VMEM((2, ny, block, v_part), BF16),
        pltpu.VMEM((2, 2, y_steps, block, v_part), BF16),
        pltpu.VMEM((2, 2, y_steps, block, v_part), BF16),
        pltpu.VMEM((2, 2, y_steps, nz, block, o_part), BF16),
        pltpu.VMEM((2, 2, y_steps, nz, block, o_part), BF16),
        pltpu.VMEM((2, nz, block, o_part), BF16),
        pltpu.VMEM((2, 2, z_steps, block, o_part), BF16),
        pltpu.VMEM((2, 2, z_steps, block, o_part), BF16),
        pltpu.VMEM((nz - 1, tw_rows, LANES), F32),
        pltpu.VMEM((ny - 1, tw_rows, LANES), F32),
        pltpu.VMEM((tw_rows, LANES), F32),
        pltpu.VMEM((2, tw_rows, LANES), F32),
        pltpu.VMEM((nz, tw_rows, LANES), F32),
        pltpu.VMEM((block, 2 * v_part + 2 * o_part), F32),
        pltpu.VMEM((own_rows, 2 * v_part + 2 * o_part), F32),
        pltpu.SemaphoreType.DMA((count,)),
        pltpu.SemaphoreType.DMA((count,)),
        pltpu.SemaphoreType.DMA,
        pltpu.SemaphoreType.DMA,
    ]
    return pl.pallas_call(
        functools.partial(sums_kernel, ny, nz),
        out_shape=(
            jax.ShapeDtypeStruct((own_rows, 2 * width), F32),
            jax.ShapeDtypeStruct((own_rows, width), F32),
            jax.ShapeDtypeStruct((tw_rows, tiles * LANES), F32),
            jax.ShapeDtypeStruct(grad_in.shape, BF16),
        ),
        in_specs=[vmem] * 5,
        out_specs=(vmem,) * 4,
        scratch_shapes=scratch,
        compiler_params=pltpu.CompilerParams(collective_id=1, has_side_effects=True),
        name="sums",
    )(c1, cg, cw, gtw, grad_in)


def sibling(value):
    count = lax.axis_size("seq")
    return lax.ppermute(value, "seq", [(k, k ^ 1) for k in range(count)])


def contract_rows(left, right):
    return lax.dot_general(left, right, (((0,), (0,)), ((), ())), preferred_element_type=F32)


def on_device(acts, cotan, proj_in, proj_out, block_mix, twiddle):
    inputs, grad_out = acts[0], cotan[0]
    w_in, w_out, square_mix = proj_in[0], proj_out[0], block_mix[0]
    tw = twiddle[0].reshape(-1, twiddle.shape[-1])
    row_count, width = inputs.shape
    ny, nz = ring_sizes(lax.axis_size("seq"))
    core = lax.rem(lax.axis_index("seq"), 2)
    half = width // 2

    def columns(value, which):
        return lax.dynamic_slice_in_dim(value, which * half, half, 1)

    inputs_2 = jnp.concatenate([inputs, sibling(inputs)], axis=0)
    cotan_2 = jnp.concatenate([columns(grad_out, core), sibling(columns(grad_out, 1 - core))], axis=0)
    projected = jnp.dot(inputs, w_in, preferred_element_type=F32).astype(BF16)
    value, gate = projected[:, :width], projected[:, width:]
    seg0 = jnp.dot(square_mix, value, preferred_element_type=F32).astype(BF16)
    d_hidden = lax.dot_general(
        grad_out, w_out, (((1,), (1,)), ((), ())), preferred_element_type=F32
    ).astype(BF16)
    gate_f = gate.astype(F32)
    dseg6 = (d_hidden.astype(F32) * gate_f).astype(BF16)
    monarch, dseg0, gtw = mixer(ny, nz, seg0, dseg6, tw)
    monarch_f = monarch.astype(F32)
    hidden = (monarch_f * gate_f).astype(BF16)
    d_gate = (d_hidden.astype(F32) * monarch_f).astype(BF16)
    mixed_out = jnp.dot(hidden, w_out, preferred_element_type=F32).astype(BF16)
    d_value = contract_rows(square_mix, dseg0).astype(BF16)
    grad_square = lax.dot_general(
        dseg0, value, (((1,), (1,)), ((), ())), preferred_element_type=F32
    )
    d_projected = jnp.concatenate([d_value, d_gate], axis=1)
    input_grad = lax.dot_general(
        d_projected, w_in, (((1,), (1,)), ((), ())), preferred_element_type=F32
    ).astype(BF16)
    hidden_2 = jnp.concatenate([hidden, sibling(hidden)], axis=0)
    d_gate_2 = jnp.concatenate([columns(d_gate, core), sibling(columns(d_gate, 1 - core))], axis=0)
    d_value_2 = jnp.concatenate([columns(d_value, core), sibling(columns(d_value, 1 - core))], axis=0)
    block = width // (ny * nz)
    cg = contract_rows(inputs_2, d_gate_2).astype(BF16).reshape(ny, nz, block, half)
    cw = contract_rows(hidden_2, cotan_2).astype(BF16).reshape(ny, nz, block, half)
    c1 = contract_rows(inputs_2, d_value_2).astype(BF16).reshape(ny, nz, block, 2, half // 2)
    c1 = jnp.transpose(c1, (3, 1, 0, 2, 4))
    win, wout, tw_grad, handed = sums(ny, nz, c1, cg, cw, gtw, input_grad)
    return (
        mixed_out[None],
        handed[None],
        win[None],
        wout[None],
        grad_square[None],
        tw_grad.reshape(twiddle.shape),
    )


def solution(mesh):
    in_specs = (
        P("pipe", "seq", None),
        P("pipe", "seq", None),
        P("pipe", None, None),
        P("pipe", None, None),
        P("pipe", "seq", None),
        P("pipe", None, None, None, None),
    )
    out_specs = (
        P("pipe", "seq", None),
        P("pipe", "seq", None),
        P("pipe", "seq", None),
        P("pipe", "seq", None),
        P("pipe", "seq", None),
        P("pipe", None, None, None, None),
    )
    return jax.shard_map(
        on_device, mesh=mesh, in_specs=in_specs, out_specs=out_specs, check_vma=False
    )
```
